256 devices in a mesh: win: 8 (over x, core), obs: 32 (over y, z).
Axes of the slice: x: 4, y: 4, z: 8, core: 2. Of those that a mesh axis runs over, the one named last changes fastest.
Arguments:
- predictors: float32 [8, 8, 1048576], P('win', None, 'obs'), may hold values from -8 to 8
- departures: float32 [8, 1048576], P('win', 'obs'), may hold values from -30 to 30
- channel: int32 [8, 1048576], P('win', 'obs'), may hold values from 0 to 299
- decay_rate: float32 [8, 300], P('win'), may hold values from 0.5 to 1
- ridge_counts: int32 [8, 300], P('win'), may hold values from 874 to 3496
Outputs:
- coefficients: float32 [8, 8, 300], P('win')
- corrected: float32 [8, 1048576], P('win', 'obs')
The draws below stay inside these ranges and needn't reach their ends.
All inputs are finite; a program needn't handle non-finite values.
Results may differ from the reference program's by a relative error of at most 0.00013.
Values sent between devices are 32-bit elements; how exact they have to be, the bound alone decides.
No kernel may reach another device: no remote copies, remote signals or barrier semaphores. Data moves between devices by JAX's collectives and lax.ppermute only.
A program may use at most 64 MiB of HBM per device.

```python
import math
import jax
import jax.numpy as jnp
from jax import lax

C = 300
K = 8
ROUNDS = 3
WINDOWS = 8
OBS = 1048576


def pick_rows(coef_table, labels):
    return jnp.take(coef_table, labels, axis=0)


def observe_world(key):
    base = jax.random.fold_in(key, 4242)
    subkeys = jax.random.split(base, 5)
    channel = jax.random.randint(subkeys[0], (WINDOWS, OBS), 0, C, dtype=jnp.int32)
    predictors = jax.random.normal(subkeys[2], (WINDOWS, K, OBS))
    noise_term = jax.random.normal(subkeys[4], (WINDOWS, OBS))
    predictors = jnp.clip(predictors, -8.0, 8.0)
    truth_table = 0.5 * jax.random.normal(subkeys[3], (WINDOWS, C, K))
    picked = jax.vmap(pick_rows)(truth_table, channel)
    signal = jnp.sum(picked * jnp.transpose(predictors, (0, 2, 1)), axis=2)
    departures = jnp.clip(signal + noise_term, -30.0, 30.0)
    return (channel, predictors.astype(jnp.float32), departures.astype(jnp.float32))


def draw_channel(key, part):
    return observe_world(key)[0]


def draw_predictors(key, part):
    return observe_world(key)[1]


def draw_departures(key, part):
    return observe_world(key)[2]


def touch_ends(values, own_key, low, top_value):
    longest = values.shape.index(max(values.shape))
    spots = []
    for shift in (0, 1):
        where = [jax.random.randint(jax.random.fold_in(own_key, axis), (), 0, length) for axis, length in enumerate(values.shape)]
        where[longest] = (where[longest] + shift) % values.shape[longest]
        spots.append(tuple(where))
    return values.at[spots[0]].set(low).at[spots[1]].set(top_value)


def levels(stream_key, extent, cuts, smallest, high):
    def one(axis_at, parts):
        steps = jax.random.uniform(jax.random.fold_in(jax.random.fold_in(stream_key, 6), axis_at), (parts,), jnp.float32, smallest / len(cuts), high / len(cuts))
        return jnp.repeat(jnp.exp(steps), extent[axis_at] // parts).reshape((-1,) + (1,) * (len(extent) - axis_at - 1))

    gain = one(*cuts[0])
    for cut in cuts[1:]:
        gain = gain * one(*cut)
    return gain


def setup_inputs(seed: int = 0) -> dict:
    arg_keys = jax.random.split(jax.random.key(seed), 6)
    predictors = draw_predictors(jax.random.fold_in(arg_keys[5], 71), 0)
    departures = draw_departures(jax.random.fold_in(arg_keys[5], 71), 0)
    channel = draw_channel(jax.random.fold_in(arg_keys[5], 71), 0)
    decay_rate = jnp.clip(jnp.exp(math.log(1.0) - 0.6931472 * jax.random.uniform(arg_keys[3], (WINDOWS, C), jnp.float32) ** levels(arg_keys[3], (WINDOWS, C), ((0, 8),), -0.2, 0.2)), 0.5, 1.0)
    ridge_counts = touch_ends(jax.random.randint(arg_keys[4], (WINDOWS, C), OBS // (4 * C) + 1, OBS // C + 2), jax.random.fold_in(arg_keys[4], 1), OBS // (4 * C) + 1, (OBS // C + 2) - 1).astype(jnp.int32)
    return {"predictors": predictors, "departures": departures, "channel": channel, "decay_rate": decay_rate, "ridge_counts": ridge_counts}


huber_edge = 1.5

def fit_rows(predictors, coeffs, channel):
    return lax.optimization_barrier(jnp.sum(predictors * jnp.take(coeffs, channel, axis=1), axis=0))

def build_features(predictors, departure, weights):
    weighted = predictors * weights[None, :]
    gram_rows = (weighted[:, None, :] * predictors[None, :, :]).reshape(-1, predictors.shape[1])
    moment_rows = weighted * departure[None, :]
    return jnp.concatenate([gram_rows, moment_rows], axis=0)

def solve_small(matrix, right_side):
    dimension = right_side.shape[0]
    factor = {}
    for column in range(dimension):
        pivot_square = matrix[column, column] - sum((factor[column, middle] * factor[column, middle] for middle in range(column)))
        pivot_root = jnp.sqrt(pivot_square)
        factor[column, column] = pivot_root
        for row_index in range(column + 1, dimension):
            partial_sum = matrix[row_index, column] - sum((factor[row_index, middle] * factor[column, middle] for middle in range(column)))
            factor[row_index, column] = partial_sum / pivot_root
    forward = []
    for row_index in range(dimension):
        entry_value = right_side[row_index] - sum((factor[row_index, middle] * forward[middle] for middle in range(row_index)))
        forward.append(entry_value / factor[row_index, row_index])
    solution = [None] * dimension
    for row_index in reversed(range(dimension)):
        entry_value = forward[row_index] - sum((factor[middle, row_index] * solution[middle] for middle in range(row_index + 1, dimension)))
        solution[row_index] = entry_value / factor[row_index, row_index]
    return jnp.stack(solution, axis=0)

def solve_channels(summed, ridges):
    dimension = K
    matrix = summed[:dimension * dimension].reshape(dimension, dimension, -1)
    matrix = matrix + ridges[None, None, :] * jnp.eye(dimension, dtype=jnp.float32)[:, :, None]
    return solve_small(matrix, summed[dimension * dimension:])

def reference(predictors, departures, channel, decay_rate, ridge_counts):
    coeffs = jnp.zeros((WINDOWS, K, C), jnp.float32)
    for round_index in range(ROUNDS):
        carried = jnp.zeros((K * K + K, C), jnp.float32)
        updated = []
        for window in range(WINDOWS):
            residual = departures[window] - fit_rows(predictors[window], coeffs[window], channel[window])
            weights = huber_edge / jnp.maximum(jnp.abs(residual), huber_edge)
            features = build_features(predictors[window], departures[window], weights)
            summed = jax.ops.segment_sum(features.T, channel[window], num_segments=C).T
            carried = decay_rate[window][None, :] * carried + summed
            updated.append(solve_channels(carried, ridge_counts[window].astype(jnp.float32)))
        coeffs = jnp.stack(updated, axis=0)
    fitted = jnp.stack([fit_rows(predictors[window], coeffs[window], channel[window]) for window in range(WINDOWS)], axis=0)
    return (coeffs, departures - fitted)
```

```python
import functools

import jax
import jax.numpy as jnp
from jax import lax
from jax.experimental import pallas as pl
from jax.experimental.pallas import tpu as pltpu
from jax.sharding import PartitionSpec as P

ROUNDS = 3
EDGE = 1.5

LANES = 128
SUB = 8
OWNERS = 32
SLOTS = 10
HALF = 5
SPLIT = HALF * OWNERS
FEATS = 48
CHUNK = 1024


def channel_row(ref):
    count = ref.shape[1]
    rows = []
    for start in range(0, 3 * LANES, LANES):
        stop = min(start + LANES, count)
        row = ref[:, start:stop].astype(jnp.float32)
        if stop - start < LANES:
            fill = jnp.ones((1, LANES - (stop - start)), jnp.float32)
            row = jnp.concatenate([row, fill], axis=1)
        rows.append(row)
    return rows


def pick(tables, index):
    low = index & (LANES - 1)
    high = index >> 7
    first, second, third = [jnp.take_along_axis(t, low, axis=1) for t in tables]
    return jnp.where(high == 0, first, jnp.where(high == 1, second, third))


def build_tables(got_ref):
    square = jnp.concatenate(
        [got_ref[...], jnp.zeros((LANES - OWNERS, LANES), jnp.float32)], axis=0
    ).T
    lane = lax.broadcasted_iota(jnp.int32, (SUB, LANES), 1)
    tables = []
    for t in range(3):
        table = jnp.zeros((SUB, LANES), jnp.float32)
        for q in range(4):
            slot = 4 * t + q
            if slot >= SLOTS:
                continue
            tile = square[slot * SUB : (slot + 1) * SUB, :]
            if q:
                tile = pltpu.roll(tile, q * OWNERS, 1)
            table = jnp.where((lane >> 5) == q, tile, table)
        tables.append(table)
    return tables


def fit(predictors, channels, tables):
    parts = []
    for g in range(predictors.shape[1] // LANES):
        at = slice(g * LANES, (g + 1) * LANES)
        index = jnp.broadcast_to(channels[:, at], (SUB, LANES))
        parts.append(predictors[:, at] * pick(tables, index))
    return jnp.sum(jnp.concatenate(parts, axis=1), axis=0, keepdims=True)


def statistics_kernel(first, *refs):
    if first:
        pred_ref, dep_ref, chan_ref, out_ref, acc_ref = refs
    else:
        pred_ref, dep_ref, chan_ref, got_ref, out_ref, acc_ref = refs
        tables = build_tables(got_ref)
    total = pred_ref.shape[1]
    acc_ref[...] = jnp.zeros_like(acc_ref)
    row_id = lax.broadcasted_iota(jnp.int32, (SPLIT, CHUNK), 0)

    def step(i, carry):
        at = pl.ds(pl.multiple_of(i * CHUNK, CHUNK), CHUNK)
        p = pred_ref[:, at]
        d = dep_ref[:, at]
        c = chan_ref[:, at]
        residual = d if first else d - fit(p, c, tables)
        weight = EDGE / jnp.maximum(jnp.abs(residual), EDGE)
        wp = p * weight
        rows = [wp * p]
        for offset in range(1, 5):
            rows.append(wp * pltpu.roll(p, SUB - offset, 0))
        rows.append(wp * d)
        feats = jnp.concatenate(rows, axis=0)
        head = feats.astype(jnp.bfloat16)
        tail = (feats - head.astype(jnp.float32)).astype(jnp.bfloat16)
        upper = c >= SPLIT
        in_upper = upper.astype(jnp.float32).astype(jnp.bfloat16)
        in_lower = 1.0 - in_upper
        columns = jnp.concatenate(
            [head * in_lower, head * in_upper, tail * in_lower, tail * in_upper], axis=0
        )
        local = jnp.where(upper, c - SPLIT, c)
        hot = (row_id == local).astype(jnp.float32).astype(jnp.bfloat16)
        acc_ref[...] += lax.dot_general(
            hot, columns, (((1,), (1,)), ((), ())), preferred_element_type=jnp.float32
        )
        return carry

    lax.fori_loop(0, total // CHUNK, step, 0)
    wide = 2 * FEATS
    sums = acc_ref[:, :wide] + acc_ref[:, wide:]
    sums = jnp.concatenate([sums, jnp.zeros((SPLIT, LANES - wide), jnp.float32)], axis=1)
    last = sums[4 * OWNERS :, :]
    lane = lax.broadcasted_iota(jnp.int32, (OWNERS, LANES), 1)
    for j in range(4):
        rows = sums[j * OWNERS : (j + 1) * OWNERS, :]
        if j < 3:
            rows = jnp.where(lane < wide, rows, pltpu.roll(last, wide - 32 * j, 1))
        out_ref[pl.ds(j, OWNERS, stride=4), :] = rows


def packed_slots():
    row = lax.broadcasted_iota(jnp.int32, (SUB, LANES), 0)
    lane = lax.broadcasted_iota(jnp.int32, (SUB, LANES), 1)
    row = row & 3
    wide = 2 * FEATS
    spilled = lane >= wide
    column = jnp.where(spilled, 32 * row + lane - wide, lane)
    j = jnp.where(spilled, 4, row)
    return jnp.where(column >= FEATS, HALF, 0) + j


def reduce_kernel(parts_ref, decay_ref, out_ref):
    owner = lax.axis_index("obs")
    summed = parts_ref[0:SUB, :]
    for t in range(1, parts_ref.shape[0] // SUB):
        summed = summed + parts_ref[t * SUB : (t + 1) * SUB, :]
    summed = summed + pltpu.roll(summed, 4, 0)
    index = jnp.minimum(packed_slots(), SLOTS - 1) * OWNERS + owner
    tables = [jnp.broadcast_to(r, (SUB, LANES)) for r in channel_row(decay_ref)]
    decay = pick(tables, index)
    row = lax.broadcasted_iota(jnp.int32, (SUB, LANES), 0)
    tile = jnp.where(row < 4, summed, decay)
    for t in range(out_ref.shape[0] // SUB):
        out_ref[t * SUB : (t + 1) * SUB, :] = tile


def solve_kernel(all_ref, ridge_ref, out_ref):
    owner = lax.axis_index("obs")
    window = lax.axis_index("win")
    row = lax.broadcasted_iota(jnp.int32, (SUB, LANES), 0)
    lane = lax.broadcasted_iota(jnp.int32, (SUB, LANES), 1)
    wide = 2 * FEATS

    carried = jnp.zeros((SUB, LANES), jnp.float32)
    kept = carried
    for w in range(all_ref.shape[0] // SUB):
        tile = all_ref[w * SUB : (w + 1) * SUB, :]
        carried = pltpu.roll(tile, 4, 0) * carried + tile
        kept = jnp.where(window == w, carried, kept)

    spilled = [
        pltpu.roll(pltpu.roll(kept, (32 * j + LANES - wide) % LANES, 1), 4 - j, 0)
        for j in range(3)
    ]
    fifth = jnp.where(lane < 32, spilled[0], jnp.where(lane < 64, spilled[1], spilled[2]))
    tile = jnp.where(row < 4, kept, jnp.where(row == 4, fifth, 0.0))
    square = jnp.concatenate(
        [tile, jnp.zeros((LANES - SUB, LANES), jnp.float32)], axis=0
    ).T
    blocks = []
    for b in range(6):
        low = square[b * SUB : (b + 1) * SUB, :]
        high = square[FEATS + b * SUB : FEATS + (b + 1) * SUB, :]
        blocks.append(jnp.where(lane < HALF, low, pltpu.roll(high, HALF, 1)))

    index = jnp.minimum(lane, SLOTS - 1) * OWNERS + owner
    ridge = pick([jnp.broadcast_to(r, (SUB, LANES)) for r in channel_row(ridge_ref)], index)

    offsets = blocks[:5]
    for d in range(5, SUB):
        offsets.append(pltpu.roll(blocks[SUB - d], SUB - d, 0))
    offsets[0] = offsets[0] + ridge
    columns = []
    for j in range(SUB):
        column = offsets[0]
        for d in range(1, SUB):
            column = jnp.where(row == (j - d) % SUB, offsets[d], column)
        columns.append(column)

    def spread(x, i):
        return jnp.broadcast_to(x[i : i + 1, :], (SUB, LANES))

    right = blocks[5]
    inverse = jnp.ones((SUB, LANES), jnp.float32)
    for j in range(SUB):
        inv = 1.0 / spread(columns[j], j)
        inverse = jnp.where(row == j, inv, inverse)
        factor = jnp.where(row > j, columns[j] * inv, 0.0)
        for k in range(j + 1, SUB):
            columns[k] = columns[k] - factor * spread(columns[k], j)
        right = right - factor * spread(right, j)
    answer = right * inverse
    for j in range(SUB - 1, 0, -1):
        factor = jnp.where(row < j, columns[j] * inverse, 0.0)
        answer = answer - factor * spread(answer, j)

    flat = jnp.take_along_axis(answer, lane >> 3, axis=1)
    flat = jnp.sum(jnp.where(row == (lane & 7), flat, 0.0), axis=0, keepdims=True)
    out_ref[...] = jnp.broadcast_to(flat, out_ref.shape)


def correct_kernel(pred_ref, dep_ref, chan_ref, got_ref, coef_ref, out_ref):
    tables = build_tables(got_ref)
    count = coef_ref.shape[1]
    for t in range(3):
        stop = min((t + 1) * LANES, count)
        coef_ref[:, t * LANES : stop] = tables[t][:, : stop - t * LANES]

    def step(i, carry):
        at = pl.ds(pl.multiple_of(i * CHUNK, CHUNK), CHUNK)
        out_ref[:, at] = dep_ref[:, at] - fit(pred_ref[:, at], chan_ref[:, at], tables)
        return carry

    lax.fori_loop(0, pred_ref.shape[1] // CHUNK, step, 0)


def call(kernel, name, out_shape, operands, scratch=()):
    vmem = pl.BlockSpec(memory_space=pltpu.VMEM)
    several = isinstance(out_shape, list)
    return pl.pallas_call(
        kernel,
        name=name,
        out_shape=out_shape,
        in_specs=[vmem] * len(operands),
        out_specs=[vmem] * len(out_shape) if several else vmem,
        scratch_shapes=list(scratch),
        compiler_params=pltpu.CompilerParams(vmem_limit_bytes=32 << 20),
    )(*operands)


def shape(*dims):
    return jax.ShapeDtypeStruct(dims, jnp.float32)


def body(predictors, departures, channel, decay_rate, ridge_counts):
    channels = decay_rate.shape[1]
    total = departures.shape[1]
    rows_here = predictors[0]
    windows = lax.axis_size("win")
    got = None
    for _ in range(ROUNDS):
        operands = [rows_here, departures, channel] + ([] if got is None else [got])
        parts = call(
            functools.partial(statistics_kernel, got is None),
            "statistics",
            shape(4 * OWNERS, LANES),
            operands,
            [pltpu.VMEM((SPLIT, 4 * FEATS), jnp.float32)],
        )
        parts = lax.all_to_all(parts, "obs", 0, 0, tiled=True)
        tile = call(reduce_kernel, "reduce", shape(windows * SUB, LANES), [parts, decay_rate])
        tiles = lax.all_to_all(tile, "win", 0, 0, tiled=True)
        flat = call(solve_kernel, "solve", shape(OWNERS, LANES), [tiles, ridge_counts])
        got = lax.all_to_all(flat, "obs", 0, 0, tiled=True)
    coeffs, corrected = call(
        correct_kernel,
        "correct",
        [shape(SUB, channels), shape(1, total)],
        [rows_here, departures, channel, got],
    )
    return (coeffs[None], corrected)


def solution(mesh):
    placed = (
        P("win", None, "obs"),
        P("win", "obs"),
        P("win", "obs"),
        P("win", None),
        P("win", None),
    )
    return jax.shard_map(
        body,
        mesh=mesh,
        in_specs=placed,
        out_specs=(P("win", None, None), P("win", "obs")),
        check_vma=False,
    )
```

```python
import functools

import jax
import jax.numpy as jnp
from jax import lax
from jax.experimental import pallas as pl
from jax.experimental.pallas import tpu as pltpu
from jax.sharding import PartitionSpec as P

ROUNDS = 3
EDGE = 1.5

LANES = 128
SUB = 8
OWNERS = 32
SLOTS = 10
HALF = 5
SPLIT = HALF * OWNERS
FEATS = 48
CHUNK = 16384


def channel_row(ref):
    count = ref.shape[1]
    rows = []
    for start in range(0, 3 * LANES, LANES):
        stop = min(start + LANES, count)
        row = ref[:, start:stop].astype(jnp.float32)
        if stop - start < LANES:
            fill = jnp.ones((1, LANES - (stop - start)), jnp.float32)
            row = jnp.concatenate([row, fill], axis=1)
        rows.append(row)
    return rows


def pick(tables, index):
    low = index & (LANES - 1)
    high = index >> 7
    first, second, third = [jnp.take_along_axis(t, low, axis=1) for t in tables]
    return jnp.where(high == 0, first, jnp.where(high == 1, second, third))


def build_tables(got_ref):
    square = jnp.concatenate(
        [got_ref[...], jnp.zeros((LANES - OWNERS, LANES), jnp.float32)], axis=0
    ).T
    lane = lax.broadcasted_iota(jnp.int32, (SUB, LANES), 1)
    tables = []
    for t in range(3):
        table = jnp.zeros((SUB, LANES), jnp.float32)
        for q in range(4):
            slot = 4 * t + q
            if slot >= SLOTS:
                continue
            tile = square[slot * SUB : (slot + 1) * SUB, :]
            if q:
                tile = pltpu.roll(tile, q * OWNERS, 1)
            table = jnp.where((lane >> 5) == q, tile, table)
        tables.append(table)
    return tables


def fit(predictors, channels, tables):
    parts = []
    for g in range(predictors.shape[1] // LANES):
        at = slice(g * LANES, (g + 1) * LANES)
        index = jnp.broadcast_to(channels[:, at], (SUB, LANES))
        parts.append(predictors[:, at] * pick(tables, index))
    return jnp.sum(jnp.concatenate(parts, axis=1), axis=0, keepdims=True)


def fetch(sources, targets, sems):
    copies = []
    for t in range(targets[0].shape[1] // CHUNK):
        at = pl.ds(t * CHUNK, CHUNK)
        chunk = [
            pltpu.make_async_copy(source.at[:, at], target.at[:, at], sems.at[t, n])
            for n, (source, target) in enumerate(zip(sources, targets))
        ]
        for copy in chunk:
            copy.start()
        copies.append(chunk)
    return copies


def statistics_kernel(first, *refs):
    if first:
        *sources, out_ref, pred_ref, dep_ref, chan_ref, sems = refs
        copies = fetch(sources, (pred_ref, dep_ref, chan_ref), sems)
    else:
        pred_ref, dep_ref, chan_ref, got_ref, out_ref = refs
        tables = build_tables(got_ref)
    row_id = lax.broadcasted_iota(jnp.int32, (SPLIT, CHUNK), 0)

    sums = jnp.zeros((4 * FEATS, SPLIT), jnp.float32)
    for start in range(0, pred_ref.shape[1], CHUNK):
        at = slice(start, start + CHUNK)
        if first:
            for copy in copies[start // CHUNK]:
                copy.wait()
        p = pred_ref[:, at]
        d = dep_ref[:, at]
        c = chan_ref[:, at]
        residual = d if first else d - fit(p, c, tables)
        weight = EDGE / jnp.maximum(jnp.abs(residual), EDGE)
        wp = p * weight
        rows = [wp * p]
        for offset in range(1, 5):
            rows.append(wp * pltpu.roll(p, SUB - offset, 0))
        rows.append(wp * d)
        feats = jnp.concatenate(rows, axis=0)
        head = feats.astype(jnp.bfloat16)
        tail = (feats - head.astype(jnp.float32)).astype(jnp.bfloat16)
        upper = c >= SPLIT
        in_upper = upper.astype(jnp.float32).astype(jnp.bfloat16)
        in_lower = 1.0 - in_upper
        columns = jnp.concatenate(
            [head * in_lower, head * in_upper, tail * in_lower, tail * in_upper], axis=0
        )
        local = jnp.where(upper, c - SPLIT, c)
        hot = (row_id == local).astype(jnp.float32).astype(jnp.bfloat16)
        sums = sums + lax.dot_general(
            columns, hot, (((1,), (1,)), ((), ())), preferred_element_type=jnp.float32
        )

    wide = 2 * FEATS
    sums = sums[:wide, :] + sums[wide:, :]
    sums = jnp.concatenate(
        [
            jnp.concatenate([sums, jnp.zeros((wide, 2 * LANES - SPLIT), jnp.float32)], axis=1),
            jnp.zeros((LANES - wide, 2 * LANES), jnp.float32),
        ],
        axis=0,
    ).T
    last = sums[4 * OWNERS : 5 * OWNERS, :]
    lane = lax.broadcasted_iota(jnp.int32, (OWNERS, LANES), 1)
    for j in range(4):
        rows = sums[j * OWNERS : (j + 1) * OWNERS, :]
        if j < 3:
            rows = jnp.where(lane < wide, rows, pltpu.roll(last, wide - 32 * j, 1))
        out_ref[pl.ds(j, OWNERS, stride=4), :] = rows


def packed_slots():
    row = lax.broadcasted_iota(jnp.int32, (SUB, LANES), 0)
    lane = lax.broadcasted_iota(jnp.int32, (SUB, LANES), 1)
    row = row & 3
    wide = 2 * FEATS
    spilled = lane >= wide
    column = jnp.where(spilled, 32 * row + lane - wide, lane)
    j = jnp.where(spilled, 4, row)
    return jnp.where(column >= FEATS, HALF, 0) + j


def reduce_kernel(parts_ref, decay_ref, out_ref):
    owner = lax.axis_index("obs")
    summed = parts_ref[0:SUB, :]
    for t in range(1, parts_ref.shape[0] // SUB):
        summed = summed + parts_ref[t * SUB : (t + 1) * SUB, :]
    summed = summed + pltpu.roll(summed, 4, 0)
    index = jnp.minimum(packed_slots(), SLOTS - 1) * OWNERS + owner
    tables = [jnp.broadcast_to(r, (SUB, LANES)) for r in channel_row(decay_ref)]
    decay = pick(tables, index)
    row = lax.broadcasted_iota(jnp.int32, (SUB, LANES), 0)
    tile = jnp.where(row < 4, summed, decay)
    for t in range(out_ref.shape[0] // SUB):
        out_ref[t * SUB : (t + 1) * SUB, :] = tile


def solve_kernel(all_ref, ridge_ref, out_ref):
    owner = lax.axis_index("obs")
    window = lax.axis_index("win")
    row = lax.broadcasted_iota(jnp.int32, (SUB, LANES), 0)
    lane = lax.broadcasted_iota(jnp.int32, (SUB, LANES), 1)
    wide = 2 * FEATS

    carried = jnp.zeros((SUB, LANES), jnp.float32)
    kept = carried
    for w in range(all_ref.shape[0] // SUB):
        tile = all_ref[w * SUB : (w + 1) * SUB, :]
        carried = pltpu.roll(tile, 4, 0) * carried + tile
        kept = jnp.where(window == w, carried, kept)

    spilled = [
        pltpu.roll(pltpu.roll(kept, (32 * j + LANES - wide) % LANES, 1), 4 - j, 0)
        for j in range(3)
    ]
    fifth = jnp.where(lane < 32, spilled[0], jnp.where(lane < 64, spilled[1], spilled[2]))
    tile = jnp.where(row < 4, kept, jnp.where(row == 4, fifth, 0.0))
    square = jnp.concatenate(
        [tile, jnp.zeros((LANES - SUB, LANES), jnp.float32)], axis=0
    ).T
    blocks = []
    for b in range(6):
        low = square[b * SUB : (b + 1) * SUB, :]
        high = square[FEATS + b * SUB : FEATS + (b + 1) * SUB, :]
        blocks.append(jnp.where(lane < HALF, low, pltpu.roll(high, HALF, 1)))

    index = jnp.minimum(lane, SLOTS - 1) * OWNERS + owner
    ridge = pick([jnp.broadcast_to(r, (SUB, LANES)) for r in channel_row(ridge_ref)], index)

    offsets = blocks[:5]
    for d in range(5, SUB):
        offsets.append(pltpu.roll(blocks[SUB - d], SUB - d, 0))
    offsets[0] = offsets[0] + ridge
    columns = []
    for j in range(SUB):
        column = offsets[0]
        for d in range(1, SUB):
            column = jnp.where(row == (j - d) % SUB, offsets[d], column)
        columns.append(column)

    def spread(x, i):
        return jnp.broadcast_to(x[i : i + 1, :], (SUB, LANES))

    right = blocks[5]
    inverse = jnp.ones((SUB, LANES), jnp.float32)
    for j in range(SUB):
        inv = 1.0 / spread(columns[j], j)
        inverse = jnp.where(row == j, inv, inverse)
        factor = jnp.where(row > j, columns[j] * inv, 0.0)
        for k in range(j + 1, SUB):
            columns[k] = columns[k] - factor * spread(columns[k], j)
        right = right - factor * spread(right, j)
    answer = right * inverse
    for j in range(SUB - 1, 0, -1):
        factor = jnp.where(row < j, columns[j] * inverse, 0.0)
        answer = answer - factor * spread(answer, j)

    flat = jnp.take_along_axis(answer, lane >> 3, axis=1)
    flat = jnp.sum(jnp.where(row == (lane & 7), flat, 0.0), axis=0, keepdims=True)
    out_ref[...] = jnp.broadcast_to(flat, out_ref.shape)


def correct_kernel(pred_ref, dep_ref, chan_ref, got_ref, coef_ref, out_ref):
    tables = build_tables(got_ref)
    count = coef_ref.shape[1]
    for t in range(3):
        stop = min((t + 1) * LANES, count)
        coef_ref[:, t * LANES : stop] = tables[t][:, : stop - t * LANES]

    for start in range(0, pred_ref.shape[1], CHUNK):
        at = slice(start, start + CHUNK)
        out_ref[:, at] = dep_ref[:, at] - fit(pred_ref[:, at], chan_ref[:, at], tables)


def call(kernel, name, out_shape, operands, scratch=(), space=pltpu.VMEM, limit=32):
    vmem = pl.BlockSpec(memory_space=pltpu.VMEM)
    several = isinstance(out_shape, list)
    return pl.pallas_call(
        kernel,
        name=name,
        out_shape=out_shape,
        in_specs=[pl.BlockSpec(memory_space=space)] * len(operands),
        out_specs=[vmem] * len(out_shape) if several else vmem,
        scratch_shapes=list(scratch),
        compiler_params=pltpu.CompilerParams(vmem_limit_bytes=limit << 20),
    )(*operands)


def shape(*dims):
    return jax.ShapeDtypeStruct(dims, jnp.float32)


def body(predictors, departures, channel, decay_rate, ridge_counts):
    channels = decay_rate.shape[1]
    total = departures.shape[1]
    rows_here = predictors[0]
    windows = lax.axis_size("win")
    got = None
    for _ in range(ROUNDS):
        operands = [rows_here, departures, channel]
        out = shape(4 * OWNERS, LANES)
        if got is None:
            scratch = [pltpu.VMEM(x.shape, x.dtype) for x in operands]
            scratch.append(pltpu.SemaphoreType.DMA((total // CHUNK, len(operands))))
            kernel = functools.partial(statistics_kernel, True)
            parts = call(kernel, "statistics", out, operands, scratch, pl.ANY, 62)
        else:
            kernel = functools.partial(statistics_kernel, False)
            parts = call(kernel, "statistics", out, [*operands, got])
        parts = lax.all_to_all(parts, "obs", 0, 0, tiled=True)
        tile = call(reduce_kernel, "reduce", shape(windows * SUB, LANES), [parts, decay_rate])
        tiles = lax.all_to_all(tile, "win", 0, 0, tiled=True)
        flat = call(solve_kernel, "solve", shape(OWNERS, LANES), [tiles, ridge_counts])
        got = lax.all_to_all(flat, "obs", 0, 0, tiled=True)
    coeffs, corrected = call(
        correct_kernel,
        "correct",
        [shape(SUB, channels), shape(1, total)],
        [rows_here, departures, channel, got],
    )
    return (coeffs[None], corrected)


def solution(mesh):
    placed = (
        P("win", None, "obs"),
        P("win", "obs"),
        P("win", "obs"),
        P("win", None),
        P("win", None),
    )
    return jax.shard_map(
        body,
        mesh=mesh,
        in_specs=placed,
        out_specs=(P("win", None, None), P("win", "obs")),
        check_vma=False,
    )
```

```python
import functools

import jax
import jax.numpy as jnp
from jax import lax
from jax.experimental import pallas as pl
from jax.experimental.pallas import tpu as pltpu
from jax.sharding import PartitionSpec as P

ROUNDS = 3
EDGE = 1.5

LANES = 128
SUB = 8
XS, CORES, YS, ZS = 4, 2, 4, 8
BLOCKS = CORES * ZS
SLOTS = 20
HALF = 10
SPLIT = HALF * BLOCKS
FEATS = 48
WIDE = 2 * FEATS
CHUNK = 16384

NEAR = [
    [(CORES * x + c) * YS * ZS + ZS * y + z for c in range(CORES) for z in range(ZS)]
    for x in range(XS)
    for y in range(YS)
]
ACROSS = [
    [(CORES * x + c) * YS * ZS + ZS * y + z for x in range(XS) for y in range(YS)]
    for c in range(CORES)
    for z in range(ZS)
]


def iotas(rows=SUB):
    row = lax.broadcasted_iota(jnp.int32, (rows, LANES), 0)
    lane = lax.broadcasted_iota(jnp.int32, (rows, LANES), 1)
    return row, lane


def take(table, index):
    return jnp.take_along_axis(table, index, axis=1, mode="promise_in_bounds")


def spread(x, i):
    return jnp.broadcast_to(x[i : i + 1, :], (SUB, LANES))


def channel_tables(ref):
    count = ref.shape[1]
    tables = []
    for start in range(0, 3 * LANES, LANES):
        stop = min(start + LANES, count)
        row = ref[:, start:stop].astype(jnp.float32)
        if stop - start < LANES:
            fill = jnp.ones((1, LANES - (stop - start)), jnp.float32)
            row = jnp.concatenate([row, fill], axis=1)
        tables.append(jnp.broadcast_to(row, (SUB, LANES)))
    return tables


def pick(tables, index):
    low = index & (LANES - 1)
    first, second, third = [take(t, low) for t in tables]
    return jnp.where(index < LANES, first, jnp.where(index < 2 * LANES, second, third))


def build_tables(got_ref):
    square = jnp.concatenate(
        [got_ref[pl.ds(r, BLOCKS, stride=2), :] for r in range(2)]
        + [jnp.zeros((LANES - 2 * BLOCKS, LANES), jnp.float32)],
        axis=0,
    ).T
    _, lane = iotas()
    tables = []
    for t in range(3):
        table = jnp.zeros((SUB, LANES), jnp.float32)
        for q in range(SUB):
            slot = SUB * t + q
            if slot >= SLOTS:
                continue
            r, s = divmod(slot, BLOCKS)
            tile = square[s * SUB : (s + 1) * SUB, :]
            shift = (q - r) * BLOCKS % LANES
            if shift:
                tile = pltpu.roll(tile, shift, 1)
            table = jnp.where((lane >> 4) == q, tile, table)
        tables.append(table)
    return tables


def fit(predictors, channels, tables):
    parts = []
    for g in range(predictors.shape[1] // LANES):
        at = slice(g * LANES, (g + 1) * LANES)
        index = jnp.broadcast_to(channels[:, at], (SUB, LANES))
        parts.append(predictors[:, at] * pick(tables, index))
    return jnp.sum(jnp.concatenate(parts, axis=1), axis=0, keepdims=True)


def block_rows(ref):
    tables = channel_tables(ref)
    row, lane = iotas()
    slot = jnp.clip(lane - WIDE, 0, SLOTS - 1)
    return jnp.concatenate(
        [pick(tables, slot * BLOCKS + row + half) for half in range(0, BLOCKS, SUB)], axis=0
    )


def statistics_kernel(first, *refs):
    if first:
        *sources, out_ref, pred_ref, dep_ref, chan_ref, decay_ref, ridge_ref, sems = refs
        targets = (pred_ref, dep_ref, chan_ref, decay_ref, ridge_ref)
        copies = [
            pltpu.make_async_copy(source, target, sems.at[n])
            for n, (source, target) in enumerate(zip(sources, targets))
        ]
        for copy in copies:
            copy.start()
        for copy in copies:
            copy.wait()
    else:
        pred_ref, dep_ref, chan_ref, decay_ref, ridge_ref, got_ref, out_ref = refs
        tables = build_tables(got_ref)
    row_id = lax.broadcasted_iota(jnp.int32, (SPLIT, CHUNK), 0)

    sums = jnp.zeros((2 * WIDE, SPLIT), jnp.float32)
    for start in range(0, pred_ref.shape[1], CHUNK):
        at = slice(start, start + CHUNK)
        p = pred_ref[:, at]
        d = dep_ref[:, at]
        c = chan_ref[:, at]
        residual = d if first else d - fit(p, c, tables)
        weight = EDGE / jnp.maximum(jnp.abs(residual), EDGE)
        wp = p * weight
        rows = [wp * p]
        for offset in range(1, 5):
            rows.append(wp * pltpu.roll(p, SUB - offset, 0))
        rows.append(wp * d)
        feats = jnp.concatenate(rows, axis=0)
        head = feats.astype(jnp.bfloat16)
        tail = (feats - head.astype(jnp.float32)).astype(jnp.bfloat16)
        upper = c >= SPLIT
        in_upper = upper.astype(jnp.float32).astype(jnp.bfloat16)
        in_lower = 1.0 - in_upper
        columns = jnp.concatenate(
            [head * in_lower, head * in_upper, tail * in_lower, tail * in_upper], axis=0
        )
        local = jnp.where(upper, c - SPLIT, c)
        hot = (row_id == local).astype(jnp.float32).astype(jnp.bfloat16)
        sums = sums + lax.dot_general(
            columns, hot, (((1,), (1,)), ((), ())), preferred_element_type=jnp.float32
        )

    sums = sums[:WIDE, :] + sums[WIDE:, :]
    sums = jnp.concatenate(
        [
            jnp.concatenate([sums, jnp.zeros((WIDE, 2 * LANES - SPLIT), jnp.float32)], axis=1),
            jnp.zeros((LANES - WIDE, 2 * LANES), jnp.float32),
        ],
        axis=0,
    ).T
    _, lane = iotas(BLOCKS)
    for j in range(SUB):
        if j < 6:
            q, third = divmod(j, 3)
            spill = sums[(SUB + q) * BLOCKS : (SUB + q + 1) * BLOCKS, :]
            spill = pltpu.roll(spill, WIDE - 32 * third, 1)
        else:
            spill = block_rows(decay_ref if j == 6 else ridge_ref)
        rows = jnp.where(lane < WIDE, sums[j * BLOCKS : (j + 1) * BLOCKS, :], spill)
        out_ref[pl.ds(j, BLOCKS, stride=SUB), :] = rows


def is_side():
    row, lane = iotas()
    return (row >= 6) & (lane >= WIDE)


def add_tiles(ref, starts):
    tiles = [ref[s : s + SUB, :] for s in starts]
    total = tiles[0]
    for tile in tiles[1:]:
        total = total + tile
    return jnp.where(is_side(), tiles[0], total)


def reduce_kernel(parts_ref, out_ref):
    for i in range(CORES):
        tile = add_tiles(parts_ref, [(i * ZS + z) * SUB for z in range(ZS)])
        for p in range(XS * YS):
            at = (p * CORES + i) * SUB
            out_ref[at : at + SUB, :] = tile


def solve_kernel(all_ref, out_ref):
    here = lax.axis_index("win") // CORES
    row, lane = iotas()

    spilled = lane >= WIDE
    third = jnp.where(row < 3, row, row - 3)
    column = jnp.where(spilled, 32 * third + lane - WIDE, lane)
    j = jnp.where(spilled, jnp.where(row < 3, SUB, SUB + 1), row)
    slot = jnp.where(column >= FEATS, HALF, 0) + j

    carried = jnp.zeros((SUB, LANES), jnp.float32)
    kept = [carried, carried]
    side = [carried, carried]
    for x in range(XS):
        for i in range(CORES):
            tile = add_tiles(all_ref, [((x * YS + y) * CORES + i) * SUB for y in range(YS)])
            carried = take(spread(tile, 6), WIDE + slot) * carried + tile
            kept[i] = jnp.where(here == x, carried, kept[i])
            side[i] = jnp.where(here == x, tile, side[i])

    tiles = []
    for i in range(CORES):
        turned = [pltpu.roll(kept[i], (32 * t + LANES - WIDE) % LANES, 1) for t in range(3)]
        extra = []
        for q in range(2):
            a, b, c = [pltpu.roll(turned[t], (q - 3 * q - t) % SUB, 0) for t in range(3)]
            extra.append(jnp.where(lane < 32, a, jnp.where(lane < 64, b, c)))
        tiles.append(kept[i])
        tiles.append(jnp.where(row == 0, extra[0], jnp.where(row == 1, extra[1], 0.0)))
    square = jnp.concatenate(
        tiles + [jnp.zeros((LANES - 2 * CORES * SUB, LANES), jnp.float32)], axis=0
    ).T
    blocks = []
    for b in range(6):
        low = square[b * SUB : (b + 1) * SUB, :]
        high = square[FEATS + b * SUB : FEATS + (b + 1) * SUB, :]
        blocks.append(jnp.where(lane < 32, low, pltpu.roll(high, 32, 1)))

    slot = jnp.where((lane & 32) == 0, 0, HALF) + jnp.minimum(lane & 15, HALF - 1)
    ridges = [take(spread(s, 7), WIDE + slot) for s in side]
    ridge = jnp.where((lane & 16) == 0, ridges[0], ridges[1])

    offsets = blocks[:5]
    for d in range(5, SUB):
        offsets.append(pltpu.roll(blocks[SUB - d], SUB - d, 0))
    offsets[0] = offsets[0] + ridge
    columns = []
    for j in range(SUB):
        column = offsets[0]
        for d in range(1, SUB):
            column = jnp.where(row == (j - d) % SUB, offsets[d], column)
        columns.append(column)

    right = blocks[5]
    inverse = jnp.ones((SUB, LANES), jnp.float32)
    for j in range(SUB):
        inv = 1.0 / spread(columns[j], j)
        inverse = jnp.where(row == j, inv, inverse)
        factor = jnp.where(row > j, columns[j] * inv, 0.0)
        for k in range(j + 1, SUB):
            columns[k] = columns[k] - factor * spread(columns[k], j)
        right = right - factor * spread(right, j)
    answer = right * inverse
    for j in range(SUB - 1, 0, -1):
        factor = jnp.where(row < j, columns[j] * inverse, 0.0)
        answer = answer - factor * spread(answer, j)

    for i in range(CORES):
        flats = []
        for r in range(2):
            slot = jnp.minimum(BLOCKS * r + (lane >> 3), SLOTS - 1)
            source = jnp.where(slot >= HALF, slot - HALF + 32, slot) + 16 * i
            flat = jnp.where(row == (lane & 7), take(answer, source), 0.0)
            flats.append(jnp.sum(flat, axis=0, keepdims=True))
        tile = jnp.where((row & 1) == 0, flats[0], flats[1])
        for half in range(2):
            at = (2 * i + half) * SUB
            out_ref[at : at + SUB, :] = tile


def correct_kernel(pred_ref, dep_ref, chan_ref, got_ref, coef_ref, out_ref):
    tables = build_tables(got_ref)
    count = coef_ref.shape[1]
    for t in range(3):
        stop = min((t + 1) * LANES, count)
        coef_ref[:, t * LANES : stop] = tables[t][:, : stop - t * LANES]

    for start in range(0, pred_ref.shape[1], CHUNK):
        at = slice(start, start + CHUNK)
        out_ref[:, at] = dep_ref[:, at] - fit(pred_ref[:, at], chan_ref[:, at], tables)


def call(kernel, name, out_shape, operands, scratch=(), space=pltpu.VMEM, limit=32):
    vmem = pl.BlockSpec(memory_space=pltpu.VMEM)
    several = isinstance(out_shape, list)
    return pl.pallas_call(
        kernel,
        name=name,
        out_shape=out_shape,
        in_specs=[pl.BlockSpec(memory_space=space)] * len(operands),
        out_specs=[vmem] * len(out_shape) if several else vmem,
        scratch_shapes=list(scratch),
        compiler_params=pltpu.CompilerParams(vmem_limit_bytes=limit << 20),
    )(*operands)


def shape(*dims):
    return jax.ShapeDtypeStruct(dims, jnp.float32)


def exchange(x, groups):
    return lax.all_to_all(
        x, ("win", "obs"), 0, 0, tiled=True, axis_index_groups=groups
    )


def body(predictors, departures, channel, decay_rate, ridge_counts):
    observed = [predictors[0], departures, channel]
    operands = [*observed, decay_rate, ridge_counts]
    total = departures.shape[1]
    out = shape(BLOCKS * SUB, LANES)
    got = None
    for _ in range(ROUNDS):
        if got is None:
            scratch = [pltpu.VMEM(x.shape, x.dtype) for x in operands]
            scratch.append(pltpu.SemaphoreType.DMA((len(operands),)))
            kernel = functools.partial(statistics_kernel, True)
            parts = call(kernel, "statistics", out, operands, scratch, pl.ANY, 62)
        else:
            kernel = functools.partial(statistics_kernel, False)
            parts = call(kernel, "statistics", out, [*operands, got])
        parts = exchange(parts, NEAR)
        pair = call(reduce_kernel, "reduce", shape(XS * YS * CORES * SUB, LANES), [parts])
        tiles = exchange(pair, ACROSS)
        flat = call(solve_kernel, "solve", shape(2 * BLOCKS, LANES), [tiles])
        got = exchange(flat, NEAR)
    coeffs, corrected = call(
        correct_kernel,
        "correct",
        [shape(SUB, decay_rate.shape[1]), shape(1, total)],
        [*observed, got],
    )
    return (coeffs[None], corrected)


def solution(mesh):
    placed = (
        P("win", None, "obs"),
        P("win", "obs"),
        P("win", "obs"),
        P("win", None),
        P("win", None),
    )
    return jax.shard_map(
        body,
        mesh=mesh,
        in_specs=placed,
        out_specs=(P("win", None, None), P("win", "obs")),
        check_vma=False,
    )
```

```python
import functools

import jax
import jax.numpy as jnp
from jax import lax
from jax.experimental import pallas as pl
from jax.experimental.pallas import tpu as pltpu
from jax.sharding import PartitionSpec as P

ROUNDS = 3
EDGE = 1.5

LANES = 128
SUB = 8
XS, CORES, YS, ZS = 4, 2, 4, 8
BLOCKS = CORES * ZS
SLOTS = 20
HALF = 10
SPLIT = HALF * BLOCKS
FEATS = 48
WIDE = 2 * FEATS
CHUNK = 16384
TILE = SUB * LANES

NEAR = [
    [(CORES * x + c) * YS * ZS + ZS * y + z for c in range(CORES) for z in range(ZS)]
    for x in range(XS)
    for y in range(YS)
]
ACROSS = [
    [(CORES * x + c) * YS * ZS + ZS * y + z for x in range(XS) for y in range(YS)]
    for c in range(CORES)
    for z in range(ZS)
]


def iotas(rows=SUB):
    row = lax.broadcasted_iota(jnp.int32, (rows, LANES), 0)
    lane = lax.broadcasted_iota(jnp.int32, (rows, LANES), 1)
    return row, lane


def take(table, index):
    return jnp.take_along_axis(table, index, axis=1, mode="promise_in_bounds")


def spread(x, i, rows=SUB):
    return jnp.broadcast_to(x[i : i + 1, :], (rows, LANES))


def channel_tables(ref):
    count = ref.shape[1]
    tables = []
    for start in range(0, 3 * LANES, LANES):
        stop = min(start + LANES, count)
        row = ref[:, start:stop].astype(jnp.float32)
        if stop - start < LANES:
            fill = jnp.ones((1, LANES - (stop - start)), jnp.float32)
            row = jnp.concatenate([row, fill], axis=1)
        tables.append(jnp.broadcast_to(row, (SUB, LANES)))
    return tables


def pick(tables, index):
    low = index & (LANES - 1)
    first, second, third = [take(t, low) for t in tables]
    return jnp.where(index < LANES, first, jnp.where(index < 2 * LANES, second, third))


def build_tables(got_ref):
    square = jnp.concatenate(
        [got_ref[pl.ds(r, BLOCKS, stride=2), :] for r in range(2)]
        + [jnp.zeros((LANES - 2 * BLOCKS, LANES), jnp.float32)],
        axis=0,
    ).T
    _, lane = iotas()
    tables = []
    for t in range(3):
        table = jnp.zeros((SUB, LANES), jnp.float32)
        for q in range(SUB):
            slot = SUB * t + q
            if slot >= SLOTS:
                continue
            r, s = divmod(slot, BLOCKS)
            tile = square[s * SUB : (s + 1) * SUB, :]
            shift = (q - r) * BLOCKS % LANES
            if shift:
                tile = pltpu.roll(tile, shift, 1)
            table = jnp.where((lane >> 4) == q, tile, table)
        tables.append(table)
    return tables


def gather_sums(tiles):
    row, _ = iotas()
    step = SUB // 2
    while step:
        low = (row & step) == 0
        half = len(tiles) // 2
        tiles = [
            jnp.where(low, a + pltpu.roll(a, SUB - step, 0), b + pltpu.roll(b, step, 0))
            for a, b in zip(tiles[:half], tiles[half:])
        ]
        step //= 2
    return tiles[0]


def fit(predictors, channels, tables):
    return gather_sums(
        [
            predictors[:, g * LANES : (g + 1) * LANES] * pick(tables, spread(channels, g))
            for g in range(SUB)
        ]
    )


def block_rows(ref):
    tables = channel_tables(ref)
    row, lane = iotas()
    slot = jnp.clip(lane - WIDE, 0, SLOTS - 1)
    return jnp.concatenate(
        [pick(tables, slot * BLOCKS + row + half) for half in range(0, BLOCKS, SUB)], axis=0
    )


def tile_of(ref, t):
    return ref[t * SUB : (t + 1) * SUB, :]


def statistics_kernel(first, *refs):
    if first:
        *sources, decay_ref, ridge_ref, out_ref, pred_ref, dep_ref, chan_ref = refs[:-3]
        decay_copy, ridge_copy, sems = refs[-3:]
        sources = [*sources, decay_ref, ridge_ref]
        targets = (pred_ref, dep_ref, chan_ref, decay_copy, ridge_copy)
        copies = [
            pltpu.make_async_copy(source, target, sems.at[n])
            for n, (source, target) in enumerate(zip(sources, targets))
        ]
        for copy in copies:
            copy.start()
        for copy in copies:
            copy.wait()
    else:
        pred_ref, dep_ref, chan_ref, got_ref, out_ref = refs
        tables = build_tables(got_ref)
    row_id = lax.broadcasted_iota(jnp.int32, (SPLIT, LANES), 0)

    sums = jnp.zeros((2 * WIDE, SPLIT), jnp.float32)
    for start in range(0, pred_ref.shape[1], CHUNK):
        columns, hots = [], []
        for t in range(start // TILE, (start + CHUNK) // TILE):
            p = pred_ref[:, t * TILE : (t + 1) * TILE]
            d = tile_of(dep_ref, t)
            c = tile_of(chan_ref, t)
            residual = d if first else d - fit(p, c, tables)
            weight = EDGE / jnp.maximum(jnp.abs(residual), EDGE)
            upper = c >= SPLIT
            local = jnp.where(upper, c - SPLIT, c)
            upper = upper.astype(jnp.float32)
            for g in range(SUB):
                pg = p[:, g * LANES : (g + 1) * LANES]
                wp = pg * spread(weight, g)
                rows = [wp * pg]
                for offset in range(1, 5):
                    rows.append(wp * pltpu.roll(pg, SUB - offset, 0))
                rows.append(wp * spread(d, g))
                feats = jnp.concatenate(rows, axis=0)
                head = feats.astype(jnp.bfloat16)
                tail = (feats - head.astype(jnp.float32)).astype(jnp.bfloat16)
                in_upper = spread(upper, g, FEATS).astype(jnp.bfloat16)
                in_lower = 1.0 - in_upper
                columns.append(
                    jnp.concatenate(
                        [head * in_lower, head * in_upper, tail * in_lower, tail * in_upper],
                        axis=0,
                    )
                )
                hot = row_id == spread(local, g, SPLIT)
                hots.append(hot.astype(jnp.float32).astype(jnp.bfloat16))
        sums = sums + lax.dot_general(
            jnp.concatenate(columns, axis=1),
            jnp.concatenate(hots, axis=1),
            (((1,), (1,)), ((), ())),
            preferred_element_type=jnp.float32,
        )

    sums = sums[:WIDE, :] + sums[WIDE:, :]
    sums = jnp.concatenate(
        [
            jnp.concatenate([sums, jnp.zeros((WIDE, 2 * LANES - SPLIT), jnp.float32)], axis=1),
            jnp.zeros((LANES - WIDE, 2 * LANES), jnp.float32),
        ],
        axis=0,
    ).T
    _, lane = iotas(BLOCKS)
    for j in range(SUB):
        if j < 6:
            q, third = divmod(j, 3)
            spill = sums[(SUB + q) * BLOCKS : (SUB + q + 1) * BLOCKS, :]
            spill = pltpu.roll(spill, WIDE - 32 * third, 1)
        elif first:
            spill = block_rows(decay_copy if j == 6 else ridge_copy)
        else:
            spill = 0.0
        rows = jnp.where(lane < WIDE, sums[j * BLOCKS : (j + 1) * BLOCKS, :], spill)
        out_ref[pl.ds(j, BLOCKS, stride=SUB), :] = rows


def is_side():
    row, lane = iotas()
    return (row >= 6) & (lane >= WIDE)


def add_tiles(ref, starts):
    tiles = [ref[s : s + SUB, :] for s in starts]
    total = tiles[0]
    for tile in tiles[1:]:
        total = total + tile
    return jnp.where(is_side(), tiles[0], total)


def reduce_kernel(parts_ref, out_ref):
    for i in range(CORES):
        tile = add_tiles(parts_ref, [(i * ZS + z) * SUB for z in range(ZS)])
        for p in range(XS * YS):
            at = (p * CORES + i) * SUB
            out_ref[at : at + SUB, :] = tile


def solve_kernel(*refs):
    all_ref, side_ref, out_ref = refs[0], refs[-2], refs[-1]
    here = lax.axis_index("win") // CORES
    row, lane = iotas()

    spilled = lane >= WIDE
    third = jnp.where(row < 3, row, row - 3)
    column = jnp.where(spilled, 32 * third + lane - WIDE, lane)
    j = jnp.where(spilled, jnp.where(row < 3, SUB, SUB + 1), row)
    slot = jnp.where(column >= FEATS, HALF, 0) + j

    carried = jnp.zeros((SUB, LANES), jnp.float32)
    kept = [carried, carried]
    side = [carried, carried]
    for x in range(XS):
        for i in range(CORES):
            starts = [((x * YS + y) * CORES + i) * SUB for y in range(YS)]
            tile = add_tiles(all_ref, starts)
            extra = side_ref[starts[0] : starts[0] + SUB, :]
            carried = take(spread(extra, 6), WIDE + slot) * carried + tile
            kept[i] = jnp.where(here == x, carried, kept[i])
            side[i] = jnp.where(here == x, extra, side[i])

    tiles = []
    for i in range(CORES):
        turned = [pltpu.roll(kept[i], (32 * t + LANES - WIDE) % LANES, 1) for t in range(3)]
        extra = []
        for q in range(2):
            a, b, c = [pltpu.roll(turned[t], (q - 3 * q - t) % SUB, 0) for t in range(3)]
            extra.append(jnp.where(lane < 32, a, jnp.where(lane < 64, b, c)))
        tiles.append(kept[i])
        tiles.append(jnp.where(row == 0, extra[0], jnp.where(row == 1, extra[1], 0.0)))
    square = jnp.concatenate(
        tiles + [jnp.zeros((LANES - 2 * CORES * SUB, LANES), jnp.float32)], axis=0
    ).T
    blocks = []
    for b in range(6):
        low = square[b * SUB : (b + 1) * SUB, :]
        high = square[FEATS + b * SUB : FEATS + (b + 1) * SUB, :]
        blocks.append(jnp.where(lane < 32, low, pltpu.roll(high, 32, 1)))

    slot = jnp.where((lane & 32) == 0, 0, HALF) + jnp.minimum(lane & 15, HALF - 1)
    ridges = [take(spread(s, 7), WIDE + slot) for s in side]
    ridge = jnp.where((lane & 16) == 0, ridges[0], ridges[1])

    offsets = blocks[:5]
    for d in range(5, SUB):
        offsets.append(pltpu.roll(blocks[SUB - d], SUB - d, 0))
    offsets[0] = offsets[0] + ridge
    columns = []
    for j in range(SUB):
        column = offsets[0]
        for d in range(1, SUB):
            column = jnp.where(row == (j - d) % SUB, offsets[d], column)
        columns.append(column)

    right = blocks[5]
    inverse = jnp.ones((SUB, LANES), jnp.float32)
    for j in range(SUB):
        inv = 1.0 / spread(columns[j], j)
        inverse = jnp.where(row == j, inv, inverse)
        factor = jnp.where(row > j, columns[j] * inv, 0.0)
        for k in range(j + 1, SUB):
            columns[k] = columns[k] - factor * spread(columns[k], j)
        right = right - factor * spread(right, j)
    answer = right * inverse
    for j in range(SUB - 1, 0, -1):
        factor = jnp.where(row < j, columns[j] * inverse, 0.0)
        answer = answer - factor * spread(answer, j)

    for i in range(CORES):
        flats = []
        for r in range(2):
            slot = jnp.minimum(BLOCKS * r + (lane >> 3), SLOTS - 1)
            source = jnp.where(slot >= HALF, slot - HALF + 32, slot) + 16 * i
            flat = jnp.where(row == (lane & 7), take(answer, source), 0.0)
            flats.append(jnp.sum(flat, axis=0, keepdims=True))
        tile = jnp.where((row & 1) == 0, flats[0], flats[1])
        for half in range(2):
            at = (2 * i + half) * SUB
            out_ref[at : at + SUB, :] = tile


def correct_kernel(pred_ref, dep_ref, chan_ref, got_ref, coef_ref, out_ref):
    tables = build_tables(got_ref)
    count = coef_ref.shape[1]
    for t in range(3):
        stop = min((t + 1) * LANES, count)
        coef_ref[:, t * LANES : stop] = tables[t][:, : stop - t * LANES]

    for t in range(pred_ref.shape[1] // TILE):
        fitted = fit(pred_ref[:, t * TILE : (t + 1) * TILE], tile_of(chan_ref, t), tables)
        out_ref[t * SUB : (t + 1) * SUB, :] = tile_of(dep_ref, t) - fitted


def call(kernel, name, out_shape, operands, scratch=(), space=pltpu.VMEM):
    vmem = pl.BlockSpec(memory_space=pltpu.VMEM)
    several = isinstance(out_shape, list)
    return pl.pallas_call(
        kernel,
        name=name,
        out_shape=out_shape,
        in_specs=[pl.BlockSpec(memory_space=space)] * len(operands),
        out_specs=[vmem] * len(out_shape) if several else vmem,
        scratch_shapes=list(scratch),
        compiler_params=pltpu.CompilerParams(vmem_limit_bytes=32 << 20),
    )(*operands)


def shape(*dims):
    return jax.ShapeDtypeStruct(dims, jnp.float32)


def exchange(x, groups):
    return lax.all_to_all(
        x, ("win", "obs"), 0, 0, tiled=True, axis_index_groups=groups
    )


def first_statistics(observed, decay_rate, ridge_counts):
    operands = [*observed, decay_rate, ridge_counts]
    scratch = [pltpu.VMEM(x.shape, x.dtype) for x in operands[3:]]
    scratch.append(pltpu.SemaphoreType.DMA((len(operands),)))
    parts, *fetched = call(
        functools.partial(statistics_kernel, True),
        "statistics",
        [shape(BLOCKS * SUB, LANES)] + [jax.ShapeDtypeStruct(x.shape, x.dtype) for x in observed],
        [pltpu.with_memory_space_constraint(x, pltpu.HBM) for x in operands],
        scratch,
        pltpu.HBM,
    )
    return parts, fetched


def body(predictors, departures, channel, decay_rate, ridge_counts):
    total = departures.shape[1]
    dense = (total // LANES, LANES)
    observed = [predictors[0], departures.reshape(dense), channel.reshape(dense)]
    parts, observed = first_statistics(observed, decay_rate, ridge_counts)
    side = []
    for index in range(ROUNDS):
        if index:
            parts = call(
                functools.partial(statistics_kernel, False),
                "statistics",
                shape(BLOCKS * SUB, LANES),
                [*observed, got],
            )
        parts = exchange(parts, NEAR)
        pair = call(reduce_kernel, "reduce", shape(XS * YS * CORES * SUB, LANES), [parts])
        tiles = exchange(pair, ACROSS)
        flat = call(solve_kernel, "solve", shape(2 * BLOCKS, LANES), [tiles, *side])
        if not index:
            side = [tiles]
        got = exchange(flat, NEAR)
    coeffs, corrected = call(
        correct_kernel,
        "correct",
        [shape(SUB, decay_rate.shape[1]), shape(*dense)],
        [*observed, got],
    )
    return (coeffs[None], corrected.reshape(1, total))


def solution(mesh):
    placed = (
        P("win", None, "obs"),
        P("win", "obs"),
        P("win", "obs"),
        P("win", None),
        P("win", None),
    )
    return jax.shard_map(
        body,
        mesh=mesh,
        in_specs=placed,
        out_specs=(P("win", None, None), P("win", "obs")),
        check_vma=False,
    )
```

```python
import functools

import jax
import jax.numpy as jnp
from jax import lax
from jax.experimental import pallas as pl
from jax.experimental.pallas import tpu as pltpu
from jax.sharding import PartitionSpec as P

ROUNDS = 3
EDGE = 1.5

LANES = 128
SUB = 8
XS, CORES, YS, ZS = 4, 2, 4, 8
BLOCKS = CORES * ZS
SLOTS = 20
HALF = 10
SPLIT = HALF * BLOCKS
FEATS = 48
WIDE = 2 * FEATS
CHUNK = 16384
TILE = SUB * LANES

NEAR = [
    [(CORES * x + c) * YS * ZS + ZS * y + z for c in range(CORES) for z in range(ZS)]
    for x in range(XS)
    for y in range(YS)
]
ACROSS = [
    [(CORES * x + c) * YS * ZS + ZS * y + z for x in range(XS) for y in range(YS)]
    for c in range(CORES)
    for z in range(ZS)
]


def iotas(rows=SUB):
    row = lax.broadcasted_iota(jnp.int32, (rows, LANES), 0)
    lane = lax.broadcasted_iota(jnp.int32, (rows, LANES), 1)
    return row, lane


def take(table, index):
    return jnp.take_along_axis(table, index, axis=1, mode="promise_in_bounds")


def spread(x, i, rows=SUB):
    return jnp.broadcast_to(x[i : i + 1, :], (rows, LANES))


def channel_tables(ref):
    count = ref.shape[1]
    tables = []
    for start in range(0, 3 * LANES, LANES):
        stop = min(start + LANES, count)
        row = ref[:, start:stop].astype(jnp.float32)
        if stop - start < LANES:
            fill = jnp.ones((1, LANES - (stop - start)), jnp.float32)
            row = jnp.concatenate([row, fill], axis=1)
        tables.append(jnp.broadcast_to(row, (SUB, LANES)))
    return tables


def pick(tables, index):
    low = index & (LANES - 1)
    first, second, third = [take(t, low) for t in tables]
    return jnp.where(index < LANES, first, jnp.where(index < 2 * LANES, second, third))


def build_tables(got_ref):
    square = jnp.concatenate(
        [got_ref[pl.ds(r, BLOCKS, stride=2), :] for r in range(2)]
        + [jnp.zeros((LANES - 2 * BLOCKS, LANES), jnp.float32)],
        axis=0,
    ).T
    _, lane = iotas()
    tables = []
    for t in range(3):
        table = jnp.zeros((SUB, LANES), jnp.float32)
        for q in range(SUB):
            slot = SUB * t + q
            if slot >= SLOTS:
                continue
            r, s = divmod(slot, BLOCKS)
            tile = square[s * SUB : (s + 1) * SUB, :]
            shift = (q - r) * BLOCKS % LANES
            if shift:
                tile = pltpu.roll(tile, shift, 1)
            table = jnp.where((lane >> 4) == q, tile, table)
        tables.append(table)
    return tables


def gather_sums(tiles):
    row, _ = iotas()
    step = SUB // 2
    while step:
        low = (row & step) == 0
        half = len(tiles) // 2
        tiles = [
            jnp.where(low, a + pltpu.roll(a, SUB - step, 0), b + pltpu.roll(b, step, 0))
            for a, b in zip(tiles[:half], tiles[half:])
        ]
        step //= 2
    return tiles[0]


def fit(predictors, channels, tables):
    return gather_sums(
        [
            predictors[:, g * LANES : (g + 1) * LANES] * pick(tables, spread(channels, g))
            for g in range(SUB)
        ]
    )


def block_rows(ref):
    tables = channel_tables(ref)
    row, lane = iotas()
    slot = jnp.clip(lane - WIDE, 0, SLOTS - 1)
    return jnp.concatenate(
        [pick(tables, slot * BLOCKS + row + half) for half in range(0, BLOCKS, SUB)], axis=0
    )


def tile_of(ref, t):
    return ref[t * SUB : (t + 1) * SUB, :]


def statistics_kernel(first, *refs):
    if first:
        *sources, decay_ref, ridge_ref, out_ref, pred_ref, dep_ref, chan_ref = refs[:-3]
        decay_copy, ridge_copy, sems = refs[-3:]
        sources = [*sources, decay_ref, ridge_ref]
        targets = (pred_ref, dep_ref, chan_ref, decay_copy, ridge_copy)
        copies = [
            pltpu.make_async_copy(source, target, sems.at[n])
            for n, (source, target) in enumerate(zip(sources, targets))
        ]
        for copy in copies:
            copy.start()
        for copy in copies:
            copy.wait()
    else:
        pred_ref, dep_ref, chan_ref, got_ref, out_ref = refs
        tables = build_tables(got_ref)
    row_id = lax.broadcasted_iota(jnp.int32, (SPLIT, LANES), 0)

    sums = jnp.zeros((2 * WIDE, SPLIT), jnp.float32)
    for start in range(0, pred_ref.shape[1], CHUNK):
        columns, hots = [], []
        for t in range(start // TILE, (start + CHUNK) // TILE):
            p = pred_ref[:, t * TILE : (t + 1) * TILE]
            d = tile_of(dep_ref, t)
            c = tile_of(chan_ref, t)
            residual = d if first else d - fit(p, c, tables)
            weight = EDGE / jnp.maximum(jnp.abs(residual), EDGE)
            upper = c >= SPLIT
            local = jnp.where(upper, c - SPLIT, c)
            upper = upper.astype(jnp.float32)
            for g in range(SUB):
                pg = p[:, g * LANES : (g + 1) * LANES]
                wp = pg * spread(weight, g)
                rows = [wp * pg]
                for offset in range(1, 5):
                    rows.append(wp * pltpu.roll(pg, SUB - offset, 0))
                rows.append(wp * spread(d, g))
                feats = jnp.concatenate(rows, axis=0)
                head = feats.astype(jnp.bfloat16)
                tail = (feats - head.astype(jnp.float32)).astype(jnp.bfloat16)
                in_upper = spread(upper, g, FEATS).astype(jnp.bfloat16)
                in_lower = 1.0 - in_upper
                columns.append(
                    jnp.concatenate(
                        [head * in_lower, head * in_upper, tail * in_lower, tail * in_upper],
                        axis=0,
                    )
                )
                hot = row_id == spread(local, g, SPLIT)
                hots.append(hot.astype(jnp.float32).astype(jnp.bfloat16))
        sums = sums + lax.dot_general(
            jnp.concatenate(columns, axis=1),
            jnp.concatenate(hots, axis=1),
            (((1,), (1,)), ((), ())),
            preferred_element_type=jnp.float32,
        )

    sums = sums[:WIDE, :] + sums[WIDE:, :]
    sums = jnp.concatenate(
        [
            jnp.concatenate([sums, jnp.zeros((WIDE, 2 * LANES - SPLIT), jnp.float32)], axis=1),
            jnp.zeros((LANES - WIDE, 2 * LANES), jnp.float32),
        ],
        axis=0,
    ).T
    _, lane = iotas(BLOCKS)
    for j in range(SUB):
        if j < 6:
            q, third = divmod(j, 3)
            spill = sums[(SUB + q) * BLOCKS : (SUB + q + 1) * BLOCKS, :]
            spill = pltpu.roll(spill, WIDE - 32 * third, 1)
        elif first:
            spill = block_rows(decay_copy if j == 6 else ridge_copy)
        else:
            spill = 0.0
        rows = jnp.where(lane < WIDE, sums[j * BLOCKS : (j + 1) * BLOCKS, :], spill)
        out_ref[pl.ds(j, BLOCKS, stride=SUB), :] = rows


def is_side():
    row, lane = iotas()
    return (row >= 6) & (lane >= WIDE)


def add_tiles(ref, starts):
    tiles = [ref[s : s + SUB, :] for s in starts]
    total = tiles[0]
    for tile in tiles[1:]:
        total = total + tile
    return jnp.where(is_side(), tiles[0], total)


def reduce_kernel(parts_ref, out_ref):
    for i in range(CORES):
        tile = add_tiles(parts_ref, [(i * ZS + z) * SUB for z in range(ZS)])
        for p in range(XS * YS):
            at = (p * CORES + i) * SUB
            out_ref[at : at + SUB, :] = tile


def solve_kernel(*refs):
    all_ref, side_ref, out_ref = refs[0], refs[-2], refs[-1]
    here = lax.axis_index("win") // CORES
    row, lane = iotas()

    spilled = lane >= WIDE
    third = jnp.where(row < 3, row, row - 3)
    column = jnp.where(spilled, 32 * third + lane - WIDE, lane)
    j = jnp.where(spilled, jnp.where(row < 3, SUB, SUB + 1), row)
    slot = jnp.where(column >= FEATS, HALF, 0) + j

    carried = jnp.zeros((SUB, LANES), jnp.float32)
    kept = [carried, carried]
    side = [carried, carried]
    for x in range(XS):
        for i in range(CORES):
            starts = [((x * YS + y) * CORES + i) * SUB for y in range(YS)]
            tile = add_tiles(all_ref, starts)
            extra = side_ref[starts[0] : starts[0] + SUB, :]
            carried = take(spread(extra, 6), WIDE + slot) * carried + tile
            kept[i] = jnp.where(here == x, carried, kept[i])
            side[i] = jnp.where(here == x, extra, side[i])

    tiles = []
    for i in range(CORES):
        turned = [pltpu.roll(kept[i], (32 * t + LANES - WIDE) % LANES, 1) for t in range(3)]
        extra = []
        for q in range(2):
            a, b, c = [pltpu.roll(turned[t], (q - 3 * q - t) % SUB, 0) for t in range(3)]
            extra.append(jnp.where(lane < 32, a, jnp.where(lane < 64, b, c)))
        tiles.append(kept[i])
        tiles.append(jnp.where(row == 0, extra[0], jnp.where(row == 1, extra[1], 0.0)))
    square = jnp.concatenate(
        tiles + [jnp.zeros((LANES - 2 * CORES * SUB, LANES), jnp.float32)], axis=0
    ).T
    blocks = []
    for b in range(6):
        low = square[b * SUB : (b + 1) * SUB, :]
        high = square[FEATS + b * SUB : FEATS + (b + 1) * SUB, :]
        blocks.append(jnp.where(lane < 32, low, pltpu.roll(high, 32, 1)))

    slot = jnp.where((lane & 32) == 0, 0, HALF) + jnp.minimum(lane & 15, HALF - 1)
    ridges = [take(spread(s, 7), WIDE + slot) for s in side]
    ridge = jnp.where((lane & 16) == 0, ridges[0], ridges[1])

    offsets = blocks[:5]
    for d in range(5, SUB):
        offsets.append(pltpu.roll(blocks[SUB - d], SUB - d, 0))
    offsets[0] = offsets[0] + ridge
    columns = []
    for j in range(SUB):
        column = offsets[0]
        for d in range(1, SUB):
            column = jnp.where(row == (j - d) % SUB, offsets[d], column)
        columns.append(column)

    columns.append(blocks[5])
    inverse = jnp.ones((SUB, LANES), jnp.float32)
    for j in range(0, SUB, 2):
        first, cross = spread(columns[j], j), spread(columns[j + 1], j)
        corner = spread(columns[j + 1], j + 1)
        inv = 1.0 / first
        ratio = cross * inv
        second = first * (1.0 / (first * corner - cross * cross))
        inverse = jnp.where(row == j, inv, jnp.where(row == j + 1, second, inverse))
        factor = jnp.where(row > j, columns[j] * inv, 0.0)
        columns[j + 1] = columns[j + 1] - factor * cross
        later = jnp.where(row > j + 1, columns[j + 1] * second, 0.0)
        for k in range(j + 2, SUB + 1):
            upper = spread(columns[k], j)
            lower = spread(columns[k], j + 1) - ratio * upper
            columns[k] = columns[k] - factor * upper - later * lower
    right = columns.pop()
    answer = right * inverse
    for j in range(SUB - 1, 0, -1):
        factor = jnp.where(row < j, columns[j] * inverse, 0.0)
        answer = answer - factor * spread(answer, j)

    for i in range(CORES):
        flats = []
        for r in range(2):
            slot = jnp.minimum(BLOCKS * r + (lane >> 3), SLOTS - 1)
            source = jnp.where(slot >= HALF, slot - HALF + 32, slot) + 16 * i
            flat = jnp.where(row == (lane & 7), take(answer, source), 0.0)
            flats.append(jnp.sum(flat, axis=0, keepdims=True))
        tile = jnp.where((row & 1) == 0, flats[0], flats[1])
        for half in range(2):
            at = (2 * i + half) * SUB
            out_ref[at : at + SUB, :] = tile


def correct_kernel(pred_ref, dep_ref, chan_ref, got_ref, coef_ref, out_ref):
    tables = build_tables(got_ref)
    count = coef_ref.shape[1]
    for t in range(3):
        stop = min((t + 1) * LANES, count)
        coef_ref[:, t * LANES : stop] = tables[t][:, : stop - t * LANES]

    for t in range(pred_ref.shape[1] // TILE):
        fitted = fit(pred_ref[:, t * TILE : (t + 1) * TILE], tile_of(chan_ref, t), tables)
        out_ref[t * SUB : (t + 1) * SUB, :] = tile_of(dep_ref, t) - fitted


def call(kernel, name, out_shape, operands, scratch=(), space=pltpu.VMEM):
    vmem = pl.BlockSpec(memory_space=pltpu.VMEM)
    several = isinstance(out_shape, list)
    return pl.pallas_call(
        kernel,
        name=name,
        out_shape=out_shape,
        in_specs=[pl.BlockSpec(memory_space=space)] * len(operands),
        out_specs=[vmem] * len(out_shape) if several else vmem,
        scratch_shapes=list(scratch),
        compiler_params=pltpu.CompilerParams(vmem_limit_bytes=32 << 20),
    )(*operands)


def shape(*dims):
    return jax.ShapeDtypeStruct(dims, jnp.float32)


def exchange(x, groups):
    return lax.all_to_all(
        x, ("win", "obs"), 0, 0, tiled=True, axis_index_groups=groups
    )


def first_statistics(observed, decay_rate, ridge_counts):
    operands = [*observed, decay_rate, ridge_counts]
    scratch = [pltpu.VMEM(x.shape, x.dtype) for x in operands[3:]]
    scratch.append(pltpu.SemaphoreType.DMA((len(operands),)))
    parts, *fetched = call(
        functools.partial(statistics_kernel, True),
        "statistics",
        [shape(BLOCKS * SUB, LANES)] + [jax.ShapeDtypeStruct(x.shape, x.dtype) for x in observed],
        [pltpu.with_memory_space_constraint(x, pltpu.HBM) for x in operands],
        scratch,
        pltpu.HBM,
    )
    return parts, fetched


def body(predictors, departures, channel, decay_rate, ridge_counts):
    total = departures.shape[1]
    dense = (total // LANES, LANES)
    observed = [predictors[0], departures.reshape(dense), channel.reshape(dense)]
    parts, observed = first_statistics(observed, decay_rate, ridge_counts)
    side = []
    for index in range(ROUNDS):
        if index:
            parts = call(
                functools.partial(statistics_kernel, False),
                "statistics",
                shape(BLOCKS * SUB, LANES),
                [*observed, got],
            )
        parts = exchange(parts, NEAR)
        pair = call(reduce_kernel, "reduce", shape(XS * YS * CORES * SUB, LANES), [parts])
        tiles = exchange(pair, ACROSS)
        flat = call(solve_kernel, "solve", shape(2 * BLOCKS, LANES), [tiles, *side])
        if not index:
            side = [tiles]
        got = exchange(flat, NEAR)
    coeffs, corrected = call(
        correct_kernel,
        "correct",
        [shape(SUB, decay_rate.shape[1]), shape(*dense)],
        [*observed, got],
    )
    return (coeffs[None], corrected.reshape(1, total))


def solution(mesh):
    placed = (
        P("win", None, "obs"),
        P("win", "obs"),
        P("win", "obs"),
        P("win", None),
        P("win", None),
    )
    return jax.shard_map(
        body,
        mesh=mesh,
        in_specs=placed,
        out_specs=(P("win", None, None), P("win", "obs")),
        check_vma=False,
    )
```

```python
import functools

import jax
import jax.numpy as jnp
from jax import lax
from jax.experimental import pallas as pl
from jax.experimental.pallas import tpu as pltpu
from jax.sharding import PartitionSpec as P

ROUNDS = 3
EDGE = 1.5

LANES = 128
SUB = 8
XS, CORES, YS, ZS = 4, 2, 4, 8
BLOCKS = CORES * ZS
SLOTS = 20
HALF = 10
SPLIT = HALF * BLOCKS
FEATS = 48
WIDE = 2 * FEATS
CHUNK = 16384
TILE = SUB * LANES

def device(x, core, y, high, low):
    return (CORES * x + core) * YS * ZS + ZS * y + 2 * high + low


NEAR = [
    [device(x, c, y, high, low) for c in range(CORES) for y in range(YS) for low in range(2)]
    for x in range(XS)
    for high in range(4)
]
ACROSS = [
    [device(x, c, y, high, low) for x in range(XS) for high in range(4)]
    for c in range(CORES)
    for y in range(YS)
    for low in range(2)
]


def iotas(rows=SUB):
    row = lax.broadcasted_iota(jnp.int32, (rows, LANES), 0)
    lane = lax.broadcasted_iota(jnp.int32, (rows, LANES), 1)
    return row, lane


def take(table, index):
    return jnp.take_along_axis(table, index, axis=1, mode="promise_in_bounds")


def spread(x, i, rows=SUB):
    return jnp.broadcast_to(x[i : i + 1, :], (rows, LANES))


def channel_tables(ref):
    count = ref.shape[1]
    tables = []
    for start in range(0, 3 * LANES, LANES):
        stop = min(start + LANES, count)
        row = ref[:, start:stop].astype(jnp.float32)
        if stop - start < LANES:
            fill = jnp.ones((1, LANES - (stop - start)), jnp.float32)
            row = jnp.concatenate([row, fill], axis=1)
        tables.append(jnp.broadcast_to(row, (SUB, LANES)))
    return tables


def pick(tables, index):
    low = index & (LANES - 1)
    first, second, third = [take(t, low) for t in tables]
    return jnp.where(index < LANES, first, jnp.where(index < 2 * LANES, second, third))


def build_tables(got_ref):
    square = jnp.concatenate(
        [got_ref[pl.ds(r, BLOCKS, stride=2), :] for r in range(2)]
        + [jnp.zeros((LANES - 2 * BLOCKS, LANES), jnp.float32)],
        axis=0,
    ).T
    _, lane = iotas()
    tables = []
    for t in range(3):
        table = jnp.zeros((SUB, LANES), jnp.float32)
        for q in range(SUB):
            slot = SUB * t + q
            if slot >= SLOTS:
                continue
            r, s = divmod(slot, BLOCKS)
            tile = square[s * SUB : (s + 1) * SUB, :]
            shift = (q - r) * BLOCKS % LANES
            if shift:
                tile = pltpu.roll(tile, shift, 1)
            table = jnp.where((lane >> 4) == q, tile, table)
        tables.append(table)
    return tables


def gather_sums(tiles):
    row, _ = iotas()
    step = SUB // 2
    while step:
        low = (row & step) == 0
        half = len(tiles) // 2
        tiles = [
            jnp.where(low, a + pltpu.roll(a, SUB - step, 0), b + pltpu.roll(b, step, 0))
            for a, b in zip(tiles[:half], tiles[half:])
        ]
        step //= 2
    return tiles[0]


def fit(predictors, channels, tables):
    return gather_sums(
        [
            predictors[:, g * LANES : (g + 1) * LANES] * pick(tables, spread(channels, g))
            for g in range(SUB)
        ]
    )


def block_rows(ref):
    tables = channel_tables(ref)
    row, lane = iotas()
    slot = jnp.clip(lane - WIDE, 0, SLOTS - 1)
    return jnp.concatenate(
        [pick(tables, slot * BLOCKS + row + half) for half in range(0, BLOCKS, SUB)], axis=0
    )


def tile_of(ref, t):
    return ref[t * SUB : (t + 1) * SUB, :]


def statistics_kernel(first, *refs):
    if first:
        *sources, decay_ref, ridge_ref, out_ref, pred_ref, dep_ref, chan_ref = refs[:-3]
        decay_copy, ridge_copy, sems = refs[-3:]
        sources = [*sources, decay_ref, ridge_ref]
        targets = (pred_ref, dep_ref, chan_ref, decay_copy, ridge_copy)
        copies = [
            pltpu.make_async_copy(source, target, sems.at[n])
            for n, (source, target) in enumerate(zip(sources, targets))
        ]
        for copy in copies:
            copy.start()
        for copy in copies:
            copy.wait()
    else:
        pred_ref, dep_ref, chan_ref, got_ref, out_ref = refs
        tables = build_tables(got_ref)
    row_id = lax.broadcasted_iota(jnp.int32, (SPLIT, LANES), 0)

    sums = jnp.zeros((2 * WIDE, SPLIT), jnp.float32)
    for start in range(0, pred_ref.shape[1], CHUNK):
        columns, hots = [], []
        for t in range(start // TILE, (start + CHUNK) // TILE):
            p = pred_ref[:, t * TILE : (t + 1) * TILE]
            d = tile_of(dep_ref, t)
            c = tile_of(chan_ref, t)
            residual = d if first else d - fit(p, c, tables)
            weight = EDGE / jnp.maximum(jnp.abs(residual), EDGE)
            upper = c >= SPLIT
            local = jnp.where(upper, c - SPLIT, c)
            upper = upper.astype(jnp.float32)
            for g in range(SUB):
                pg = p[:, g * LANES : (g + 1) * LANES]
                wp = pg * spread(weight, g)
                rows = [wp * pg]
                for offset in range(1, 5):
                    rows.append(wp * pltpu.roll(pg, SUB - offset, 0))
                rows.append(wp * spread(d, g))
                feats = jnp.concatenate(rows, axis=0)
                head = feats.astype(jnp.bfloat16)
                tail = (feats - head.astype(jnp.float32)).astype(jnp.bfloat16)
                in_upper = spread(upper, g, FEATS).astype(jnp.bfloat16)
                in_lower = 1.0 - in_upper
                columns.append(
                    jnp.concatenate(
                        [head * in_lower, head * in_upper, tail * in_lower, tail * in_upper],
                        axis=0,
                    )
                )
                hot = row_id == spread(local, g, SPLIT)
                hots.append(hot.astype(jnp.float32).astype(jnp.bfloat16))
        sums = sums + lax.dot_general(
            jnp.concatenate(columns, axis=1),
            jnp.concatenate(hots, axis=1),
            (((1,), (1,)), ((), ())),
            preferred_element_type=jnp.float32,
        )

    sums = sums[:WIDE, :] + sums[WIDE:, :]
    sums = jnp.concatenate(
        [
            jnp.concatenate([sums, jnp.zeros((WIDE, 2 * LANES - SPLIT), jnp.float32)], axis=1),
            jnp.zeros((LANES - WIDE, 2 * LANES), jnp.float32),
        ],
        axis=0,
    ).T
    _, lane = iotas(BLOCKS)
    for j in range(SUB):
        if j < 6:
            q, third = divmod(j, 3)
            spill = sums[(SUB + q) * BLOCKS : (SUB + q + 1) * BLOCKS, :]
            spill = pltpu.roll(spill, WIDE - 32 * third, 1)
        elif first:
            spill = block_rows(decay_copy if j == 6 else ridge_copy)
        else:
            spill = 0.0
        rows = jnp.where(lane < WIDE, sums[j * BLOCKS : (j + 1) * BLOCKS, :], spill)
        out_ref[pl.ds(j, BLOCKS, stride=SUB), :] = rows


def is_side():
    row, lane = iotas()
    return (row >= 6) & (lane >= WIDE)


def add_tiles(ref, starts):
    tiles = [ref[s : s + SUB, :] for s in starts]
    total = tiles[0]
    for tile in tiles[1:]:
        total = total + tile
    return jnp.where(is_side(), tiles[0], total)


def reduce_kernel(parts_ref, out_ref):
    for i in range(CORES):
        tile = add_tiles(parts_ref, [(i * ZS + z) * SUB for z in range(ZS)])
        for p in range(XS * YS):
            at = (p * CORES + i) * SUB
            out_ref[at : at + SUB, :] = tile


def solve_kernel(*refs):
    all_ref, side_ref, out_ref = refs[0], refs[-2], refs[-1]
    here = lax.axis_index("win") // CORES
    row, lane = iotas()

    spilled = lane >= WIDE
    third = jnp.where(row < 3, row, row - 3)
    column = jnp.where(spilled, 32 * third + lane - WIDE, lane)
    j = jnp.where(spilled, jnp.where(row < 3, SUB, SUB + 1), row)
    slot = jnp.where(column >= FEATS, HALF, 0) + j

    carried = jnp.zeros((SUB, LANES), jnp.float32)
    kept = [carried, carried]
    side = [carried, carried]
    for x in range(XS):
        for i in range(CORES):
            starts = [((x * YS + y) * CORES + i) * SUB for y in range(YS)]
            tile = add_tiles(all_ref, starts)
            extra = side_ref[starts[0] : starts[0] + SUB, :]
            carried = take(spread(extra, 6), WIDE + slot) * carried + tile
            kept[i] = jnp.where(here == x, carried, kept[i])
            side[i] = jnp.where(here == x, extra, side[i])

    tiles = []
    for i in range(CORES):
        turned = [pltpu.roll(kept[i], (32 * t + LANES - WIDE) % LANES, 1) for t in range(3)]
        extra = []
        for q in range(2):
            a, b, c = [pltpu.roll(turned[t], (q - 3 * q - t) % SUB, 0) for t in range(3)]
            extra.append(jnp.where(lane < 32, a, jnp.where(lane < 64, b, c)))
        tiles.append(kept[i])
        tiles.append(jnp.where(row == 0, extra[0], jnp.where(row == 1, extra[1], 0.0)))
    square = jnp.concatenate(
        tiles + [jnp.zeros((LANES - 2 * CORES * SUB, LANES), jnp.float32)], axis=0
    ).T
    blocks = []
    for b in range(6):
        low = square[b * SUB : (b + 1) * SUB, :]
        high = square[FEATS + b * SUB : FEATS + (b + 1) * SUB, :]
        blocks.append(jnp.where(lane < 32, low, pltpu.roll(high, 32, 1)))

    slot = jnp.where((lane & 32) == 0, 0, HALF) + jnp.minimum(lane & 15, HALF - 1)
    ridges = [take(spread(s, 7), WIDE + slot) for s in side]
    ridge = jnp.where((lane & 16) == 0, ridges[0], ridges[1])

    offsets = blocks[:5]
    for d in range(5, SUB):
        offsets.append(pltpu.roll(blocks[SUB - d], SUB - d, 0))
    offsets[0] = offsets[0] + ridge
    columns = []
    for j in range(SUB):
        column = offsets[0]
        for d in range(1, SUB):
            column = jnp.where(row == (j - d) % SUB, offsets[d], column)
        columns.append(column)

    columns.append(blocks[5])
    inverse = jnp.ones((SUB, LANES), jnp.float32)
    for j in range(0, SUB, 2):
        first, cross = spread(columns[j], j), spread(columns[j + 1], j)
        corner = spread(columns[j + 1], j + 1)
        inv = 1.0 / first
        ratio = cross * inv
        second = first * (1.0 / (first * corner - cross * cross))
        inverse = jnp.where(row == j, inv, jnp.where(row == j + 1, second, inverse))
        factor = jnp.where(row > j, columns[j] * inv, 0.0)
        columns[j + 1] = columns[j + 1] - factor * cross
        later = jnp.where(row > j + 1, columns[j + 1] * second, 0.0)
        for k in range(j + 2, SUB + 1):
            upper = spread(columns[k], j)
            lower = spread(columns[k], j + 1) - ratio * upper
            columns[k] = columns[k] - factor * upper - later * lower
    right = columns.pop()
    answer = right * inverse
    for j in range(SUB - 1, 0, -1):
        factor = jnp.where(row < j, columns[j] * inverse, 0.0)
        answer = answer - factor * spread(answer, j)

    for i in range(CORES):
        flats = []
        for r in range(2):
            slot = jnp.minimum(BLOCKS * r + (lane >> 3), SLOTS - 1)
            source = jnp.where(slot >= HALF, slot - HALF + 32, slot) + 16 * i
            flat = jnp.where(row == (lane & 7), take(answer, source), 0.0)
            flats.append(jnp.sum(flat, axis=0, keepdims=True))
        tile = jnp.where((row & 1) == 0, flats[0], flats[1])
        for half in range(2):
            at = (2 * i + half) * SUB
            out_ref[at : at + SUB, :] = tile


def correct_kernel(pred_ref, dep_ref, chan_ref, got_ref, coef_ref, out_ref):
    tables = build_tables(got_ref)
    count = coef_ref.shape[1]
    for t in range(3):
        stop = min((t + 1) * LANES, count)
        coef_ref[:, t * LANES : stop] = tables[t][:, : stop - t * LANES]

    for t in range(pred_ref.shape[1] // TILE):
        fitted = fit(pred_ref[:, t * TILE : (t + 1) * TILE], tile_of(chan_ref, t), tables)
        out_ref[t * SUB : (t + 1) * SUB, :] = tile_of(dep_ref, t) - fitted


def call(kernel, name, out_shape, operands, scratch=(), space=pltpu.VMEM):
    vmem = pl.BlockSpec(memory_space=pltpu.VMEM)
    several = isinstance(out_shape, list)
    return pl.pallas_call(
        kernel,
        name=name,
        out_shape=out_shape,
        in_specs=[pl.BlockSpec(memory_space=space)] * len(operands),
        out_specs=[vmem] * len(out_shape) if several else vmem,
        scratch_shapes=list(scratch),
        compiler_params=pltpu.CompilerParams(vmem_limit_bytes=32 << 20),
    )(*operands)


def shape(*dims):
    return jax.ShapeDtypeStruct(dims, jnp.float32)


def exchange(x, groups):
    return lax.all_to_all(
        x, ("win", "obs"), 0, 0, tiled=True, axis_index_groups=groups
    )


def first_statistics(observed, decay_rate, ridge_counts):
    operands = [*observed, decay_rate, ridge_counts]
    scratch = [pltpu.VMEM(x.shape, x.dtype) for x in operands[3:]]
    scratch.append(pltpu.SemaphoreType.DMA((len(operands),)))
    parts, *fetched = call(
        functools.partial(statistics_kernel, True),
        "statistics",
        [shape(BLOCKS * SUB, LANES)] + [jax.ShapeDtypeStruct(x.shape, x.dtype) for x in observed],
        [pltpu.with_memory_space_constraint(x, pltpu.HBM) for x in operands],
        scratch,
        pltpu.HBM,
    )
    return parts, fetched


def body(predictors, departures, channel, decay_rate, ridge_counts):
    total = departures.shape[1]
    dense = (total // LANES, LANES)
    observed = [predictors[0], departures.reshape(dense), channel.reshape(dense)]
    parts, observed = first_statistics(observed, decay_rate, ridge_counts)
    side = []
    for index in range(ROUNDS):
        if index:
            parts = call(
                functools.partial(statistics_kernel, False),
                "statistics",
                shape(BLOCKS * SUB, LANES),
                [*observed, got],
            )
        parts = exchange(parts, NEAR)
        pair = call(reduce_kernel, "reduce", shape(XS * YS * CORES * SUB, LANES), [parts])
        tiles = exchange(pair, ACROSS)
        flat = call(solve_kernel, "solve", shape(2 * BLOCKS, LANES), [tiles, *side])
        if not index:
            side = [tiles]
        got = exchange(flat, NEAR)
    coeffs, corrected = call(
        correct_kernel,
        "correct",
        [shape(SUB, decay_rate.shape[1]), shape(*dense)],
        [*observed, got],
    )
    return (coeffs[None], corrected.reshape(1, total))


def solution(mesh):
    placed = (
        P("win", None, "obs"),
        P("win", "obs"),
        P("win", "obs"),
        P("win", None),
        P("win", None),
    )
    return jax.shard_map(
        body,
        mesh=mesh,
        in_specs=placed,
        out_specs=(P("win", None, None), P("win", "obs")),
        check_vma=False,
    )
```
